256 devices in a mesh: chan: 32 (over z, y_hi, core), tm: 8 (over y_lo, x).
Axes of the slice: x: 4, y: 4 (y_hi: 2, y_lo: 2; y = y_hi * 2 + y_lo), z: 8, core: 2. Of those that a mesh axis runs over, the one named last changes fastest.
Arguments:
- traces: bfloat16 [32, 192, 128, 1024], P('chan', 'tm'), may hold values from -6 to 6
- valid_mask: int32 [32, 192, 1024], P('chan', 'tm'), may hold values 0 or 1
- pair_owner: int32 [32, 4], P('chan'), may hold values from -1 to 31, as said below
Outputs:
- correlations: float32 [32, 4, 101, 128], P('chan')
The draws below stay inside these ranges and needn't reach their ends.
Inputs may be any that keep to these rules, and one draw needn't show every extreme that they name: `pair_owner`: row r lists distinct owners in r + 1 .. r + 4 (within the cable) in its leading slots, then -1; every reader with a block above it has one pair or more, and reader 0 fills all 4 slots.
All inputs are finite; a program needn't handle non-finite values. No bound on the sum of `valid_mask` on one device may be relied on, other than what follows from the above.
Results may differ from the reference program's by a relative error of at most 0.0052.
Values may be sent and summed in bfloat16 or wider, within the bound.
No kernel may reach another device: no remote copies, remote signals or barrier semaphores. Data moves between devices by JAX's collectives and lax.ppermute only.
A program may use at most 64 MiB of HBM per device.

```python
import math
import jax
import jax.numpy as jnp
from jax import lax

BLOCK = 128
WIN = 1024
NF = 256
MAXLAG = 50
SMOOTH = 4
REACH = 4
BLOCKS = 32
WINDOWS = 192
LAGS = 101


def draw_pair_owner(key, part):
    key_order, key_count = jax.random.split(jax.random.fold_in(key, 11))
    reader = jnp.arange(BLOCKS, dtype=jnp.int32)[:, None]
    steps = jnp.arange(1, REACH + 1, dtype=jnp.int32)[None, :]
    inside = reader + steps < BLOCKS
    scores = jax.random.randint(key_order, (BLOCKS, REACH), 0, 1 << 16, dtype=jnp.int32) * REACH + (steps - 1)
    biggest = (1 << 16) * REACH + REACH
    scores = jnp.where(inside, scores, biggest)
    order = jnp.argsort(scores, axis=1, stable=True)
    picked = jnp.take_along_axis(jnp.broadcast_to(steps, (BLOCKS, REACH)), order, axis=1)
    available = jnp.sum(inside.astype(jnp.int32), axis=1)
    counts = jax.random.randint(key_count, (BLOCKS,), 1, REACH + 1, dtype=jnp.int32)
    counts = jnp.where(jnp.arange(BLOCKS, dtype=jnp.int32) == 0, REACH, counts)
    counts = jnp.minimum(counts, available)
    slots = jnp.arange(REACH, dtype=jnp.int32)[None, :]
    owner = jnp.where(slots < counts[:, None], reader + picked, -1)
    return owner.astype(jnp.int32)


def set_ends(result, key, smallest, top_value):
    shape = result.shape
    index_at = [jax.random.randint(jax.random.fold_in(key, axis), (), 0, shape[axis]) for axis in range(len(shape))]
    result = result.at[tuple(index_at)].set(smallest)
    longest = shape.index(max(shape))
    index_at[longest] = (index_at[longest] + 1) % shape[longest]
    return result.at[tuple(index_at)].set(top_value)


def levels(key, dims, shards, smallest, high):
    gain = 1.0
    for axis_at, parts in shards:
        steps = jax.random.uniform(jax.random.fold_in(jax.random.fold_in(key, 6), axis_at), (parts,), jnp.float32, smallest / len(shards), high / len(shards))
        gain = gain * jnp.repeat(jnp.exp(steps), dims[axis_at] // parts).reshape((-1,) + (1,) * (len(dims) - 1 - axis_at))
    return gain


def scatter_about(key, dims, width, most, cuts=(), held_as=jnp.bfloat16):
    drawn = width * jax.random.normal(key, dims, jnp.float32)
    if cuts:
        drawn = drawn * levels(key, dims, cuts, -0.22, 0.18)
    return jnp.clip(drawn, -most, most).astype(held_as)


def setup_inputs(seed: int = 0) -> dict:
    seeds = jax.random.split(jax.random.key(seed), 4)
    return {
        "traces": scatter_about(seeds[0], (BLOCKS, WINDOWS, BLOCK, WIN), 1.0, 6.0, ((0, 32), (1, 8))),
        "valid_mask": set_ends((jax.random.randint(seeds[1], (BLOCKS, WINDOWS, WIN), 0, 8) < 7).astype(jnp.int32), jax.random.fold_in(seeds[1], 1), 0, 1),
        "pair_owner": draw_pair_owner(jax.random.fold_in(seeds[3], 71), 0),
    }


water_level = 0.05
eps = 1e-06

def forward_table():
    samples = jnp.arange(WIN, dtype=jnp.int32)
    bins = jnp.arange(1, NF + 1, dtype=jnp.int32)
    phase = samples[:, None] * bins[None, :] % WIN
    angle = phase.astype(jnp.float32) * jnp.float32(2.0 * math.pi / WIN)
    return jnp.concatenate([jnp.cos(angle), -jnp.sin(angle)], axis=1).astype(jnp.bfloat16)

def inverse_table():
    bins = jnp.arange(1, NF + 1, dtype=jnp.int32)
    offsets = jnp.arange(LAGS, dtype=jnp.int32) - MAXLAG
    phase = bins[:, None] * offsets[None, :] % WIN
    angle = phase.astype(jnp.float32) * jnp.float32(2.0 * math.pi / WIN)
    factor = jnp.float32(1.0 / math.sqrt(WINDOWS * NF))
    return jnp.concatenate([jnp.cos(angle), -jnp.sin(angle)], axis=0) * factor

def whiten(block_traces, block_mask, forward):
    masked = block_traces * block_mask[:, None, :].astype(jnp.bfloat16)
    wins, chans, samples = masked.shape
    spectra = jnp.dot(masked.reshape(wins * chans, samples), forward, preferred_element_type=jnp.float32)
    spectra = spectra.reshape(wins, chans, 2 * NF)
    real_part = spectra[..., :NF]
    imag_part = spectra[..., NF:]
    amplitude = jnp.sqrt(real_part * real_part + imag_part * imag_part)
    padded = jnp.pad(amplitude, ((0, 0), (0, 0), (SMOOTH, SMOOTH)))
    smooth = padded[..., 0:NF]
    for j in range(1, 2 * SMOOTH + 1):
        smooth = smooth + padded[..., j:j + NF]
    smooth = smooth / jnp.float32(2 * SMOOTH + 1)
    divisor = smooth + water_level * lax.optimization_barrier(jnp.mean(amplitude, axis=-1, keepdims=True)) + eps
    return (spectra / jnp.concatenate([divisor, divisor], axis=-1)).astype(jnp.bfloat16)

def cross_spectrum(own_spec, other_spec):
    left = own_spec.astype(jnp.float32)
    right = other_spec.astype(jnp.float32)
    swapped = jnp.concatenate([right[..., NF:], right[..., :NF]], axis=-1)
    direct = jnp.einsum('wcf,wcf->cf', left, right)
    crossed = jnp.einsum('wcf,wcf->cf', left, swapped)
    return jnp.concatenate([direct[:, :NF] + direct[:, NF:], crossed[:, :NF] - crossed[:, NF:]], axis=-1)

def reference(traces, valid_mask, pair_owner):
    forward = forward_table()
    inverse = inverse_table()
    white_all = lax.map(lambda item: whiten(item[0], item[1], forward), (traces, valid_mask))

    def one_reader(reader):
        own_spec = white_all[reader]
        owners = pair_owner[reader]
        stacks = []
        for slot in range(REACH):
            owner = owners[slot]
            other = white_all[jnp.maximum(owner, 0)]
            keep = (owner >= 0).astype(jnp.float32)
            stacks.append(cross_spectrum(own_spec, other) * keep)
        cross = jnp.stack(stacks, axis=0)
        return jnp.einsum('pck,kl->plc', cross, inverse, precision=lax.Precision.HIGHEST)
    return lax.map(one_reader, jnp.arange(BLOCKS, dtype=jnp.int32))
```

```python
import functools
import math

import jax
import jax.numpy as jnp
import numpy as np
from jax import lax
from jax.experimental import pallas as pl
from jax.experimental.pallas import tpu as pltpu
from jax.sharding import PartitionSpec as P

NF = 256
WIN = 1024
MAXLAG = 50
SMOOTH = 4
REACH = 4
LAGS = 2 * MAXLAG + 1
ROWS = 104
TABLE_ROWS = 112
HALF = 64
STEP = 3
TILE = 16
PAIRS = 8
SLOTS = 9
CHUNKS = ((0, 6), (6, 12), (18, 6))
WATER = 0.05
EPS = 1e-06


f32 = jnp.float32
bf16 = jnp.bfloat16


def forward_table():
    samples = np.arange(WIN, dtype=np.int32)
    bins = np.arange(1, NF + 1, dtype=np.int32)
    phase = samples[:, None] * bins[None, :] % WIN
    angle = phase.astype(np.float32) * np.float32(2.0 * math.pi / WIN)
    return np.concatenate([np.cos(angle), -np.sin(angle)], axis=1).astype(bf16)


def inverse_tables(windows_all):
    bins = np.arange(1, NF + 1, dtype=np.int32)
    offsets = np.arange(LAGS, dtype=np.int32) - MAXLAG
    phase = bins[None, :] * offsets[:, None] % WIN
    angle = phase.astype(np.float32) * np.float32(2.0 * math.pi / WIN)
    factor = np.float32(1.0 / math.sqrt(windows_all * NF))
    table = np.concatenate([np.cos(angle), -np.sin(angle)], axis=1) * factor
    table = np.pad(table, ((0, TABLE_ROWS - LAGS), (0, 0))).astype(np.float32)
    high = table.astype(bf16)
    low = (table - high.astype(np.float32)).astype(bf16)
    return high, low


def band_table():
    bins = np.arange(NF)
    near = np.abs(bins[:, None] - bins[None, :]) <= SMOOTH
    return np.concatenate([near, near], axis=0).astype(bf16)


def whiten_kernel(first, role, traces, mask, forward, band, big, small, both, masked, spectra, split, level):
    step = pl.program_id(0)
    y_hi = role[0]
    for j in range(STEP):
        keep = mask[pl.ds(first + step * STEP + j, 1), :].astype(f32).astype(bf16)
        for h in range(2):
            half = y_hi if h == 0 else 1 - y_hi
            rows = pl.ds(pl.multiple_of(half * HALF, HALF), HALF)
            masked[pl.ds((h * STEP + j) * HALF, HALF), :] = traces[j, rows, :] * keep
    spectra[...] = jnp.dot(masked[...], forward[...], preferred_element_type=f32)
    for r in range(0, 2 * STEP * HALF, 32):
        rows = slice(r, r + 32)
        real = spectra[rows, :NF]
        imag = spectra[rows, NF:]
        amplitude = jnp.sqrt(real * real + imag * imag)
        high = amplitude.astype(bf16)
        split[rows, :NF] = high
        split[rows, NF:] = (amplitude - high.astype(f32)).astype(bf16)
        total = jnp.sum(amplitude, axis=-1, keepdims=True)
        level[rows, :] = jnp.broadcast_to(total * f32(WATER / NF) + f32(EPS), (32, 128))
    smooth = jnp.dot(split[...], band[...], preferred_element_type=f32)
    for r in range(0, 2 * STEP * HALF, 32):
        rows = slice(r, r + 32)
        base = level[rows, :]
        divisor = smooth[rows, :] * f32(1.0 / (2 * SMOOTH + 1)) + jnp.concatenate([base, base], axis=1)
        inverse = 1.0 / divisor
        real = (spectra[rows, :NF] * inverse).astype(bf16)
        imag = (spectra[rows, NF:] * inverse).astype(bf16)
        h, rest = divmod(r, STEP * HALF)
        j, c = divmod(rest, HALF)
        out = big if h == 0 else small
        out[j, c : c + 32, :NF] = real
        out[j, c : c + 32, NF:] = imag
        both[h, j, c : c + 32, :NF] = real
        both[h, j, c : c + 32, NF:] = imag


def whiten(role, traces, mask, forward, band, first, count):
    rows = 2 * STEP * HALF
    base = first // STEP
    part = jax.ShapeDtypeStruct((count, HALF, 2 * NF), bf16)
    return pl.pallas_call(
        functools.partial(whiten_kernel, first),
        grid_spec=pltpu.PrefetchScalarGridSpec(
            num_scalar_prefetch=1,
            grid=(count // STEP,),
            in_specs=[
                pl.BlockSpec((STEP, 2 * HALF, WIN), lambda i, role: (base + i, 0, 0)),
                pl.BlockSpec(mask.shape, lambda i, role: (0, 0)),
                pl.BlockSpec(forward.shape, lambda i, role: (0, 0)),
                pl.BlockSpec(band.shape, lambda i, role: (0, 0)),
            ],
            out_specs=[
                pl.BlockSpec((STEP, HALF, 2 * NF), lambda i, role: (i, 0, 0)),
                pl.BlockSpec((STEP, HALF, 2 * NF), lambda i, role: (i, 0, 0)),
                pl.BlockSpec((2, STEP, HALF, 2 * NF), lambda i, role: (0, i, 0, 0)),
            ],
            scratch_shapes=[
                pltpu.VMEM((rows, WIN), bf16),
                pltpu.VMEM((rows, 2 * NF), f32),
                pltpu.VMEM((rows, 2 * NF), bf16),
                pltpu.VMEM((rows, 128), f32),
            ],
        ),
        out_shape=[part, part, jax.ShapeDtypeStruct((2, count, HALF, 2 * NF), bf16)],
        cost_estimate=pl.CostEstimate(
            flops=2 * count * 2 * HALF * (WIN * 2 * NF + 2 * NF * NF),
            bytes_accessed=count * 2 * HALF * (WIN + 4 * NF) * 2,
            transcendentals=count * 2 * HALF * NF * 2,
        ),
        name=f"whiten_{first}",
    )(role, traces, mask, forward, band)


def cross_kernel(count, start, last, role, *refs):
    own_big, own_small, other_own, near_big, near_small, across, other_big, other_small, other_across = refs[:9]
    refs = refs[9:]
    before = None
    if not start:
        before, refs = refs[0], refs[1:]
    if last:
        table_high, table_low, full, to_y, to_z, buf, sem, total = refs
    else:
        total, buf, sem = refs
    y_hi = role[0]
    core = role[1]

    def copy(source, t, slot):
        return pltpu.make_async_copy(source.at[:, pl.ds(t * TILE, TILE), :], buf.at[t, slot], sem.at[t, slot])

    other_own_big = other_own.at[0]
    other_own_small = other_own.at[1]
    tiles = HALF // TILE
    for t in range(tiles):
        copy(across, t, 2).start()
        copy(other_across, t, 4).start()
        copy(other_own_big, t, 5).start()

        @pl.when(y_hi == 0)
        def _():
            copy(own_big, t, 0).start()
            copy(near_big, t, 1).start()
            copy(other_big, t, 3).start()
            copy(near_small, t, 6).start()
            copy(own_small, t, 7).start()
            copy(other_own_small, t, 8).start()

        @pl.when(y_hi != 0)
        def _():
            copy(near_big, t, 0).start()
            copy(own_big, t, 1).start()
            copy(other_own_big, t, 3).start()
            copy(own_small, t, 6).start()
            copy(near_small, t, 7).start()

        @pl.when((y_hi != 0) & (core == 0))
        def _():
            copy(other_own_small, t, 8).start()

        @pl.when((y_hi != 0) & (core != 0))
        def _():
            copy(other_small, t, 8).start()

    reader_5 = jnp.where((y_hi != 0) & (core == 0), 1, 0)
    owner_5 = jnp.where((y_hi == 0) & (core == 0), 5, 3)
    reader_7 = jnp.where((y_hi == 0) & (core == 0), 7, 6)

    def tile(t, carry):
        for slot in range(SLOTS):
            copy(across, t, slot).wait()
        rows = pl.ds(pl.multiple_of(t * TILE, TILE), TILE)
        for f in range(0, NF, 128):
            re = slice(f, f + 128)
            im = slice(NF + f, NF + f + 128)

            def run(slots, pairs):
                def begin(index):
                    if start:
                        return jnp.zeros((TILE, 128), f32), jnp.zeros((TILE, 128), f32)
                    return before[index, rows, re], before[index, rows, im]

                def window(w, sums):
                    at = [(buf[t, s, w, :, re].astype(f32), buf[t, s, w, :, im].astype(f32)) for s in slots]
                    out = []
                    for (index, a, b), (sr, si) in zip(pairs, sums):
                        ar, ai = at[a]
                        br, bi = at[b]
                        out.append((sr + (ar * br + ai * bi), si + (ar * bi - ai * br)))
                    return tuple(out)

                sums = lax.fori_loop(0, count, window, tuple(begin(p[0]) for p in pairs), unroll=3)
                for (index, _, _), (sr, si) in zip(pairs, sums):
                    total[index, rows, re] = sr
                    total[index, rows, im] = si

            run((0, 1, 2, 3, 4), ((0, 0, 2), (1, 0, 4), (2, 0, 1), (6, 2, 1), (7, 2, 3)))
            run((reader_5, owner_5, 6, 7, reader_7, 8), ((3, 0, 1), (4, 2, 3), (5, 4, 5)))
        return carry

    lax.fori_loop(0, tiles, tile, 0)
    if last:
        stack = total[...].reshape(PAIRS * HALF, 2 * NF)
        high = stack.astype(bf16)
        low = (stack - high.astype(f32)).astype(bf16)
        dims = (((1,), (1,)), ((), ()))
        dot = functools.partial(lax.dot_general, dimension_numbers=dims, preferred_element_type=f32)
        result = dot(table_high[...], high) + dot(table_high[...], low) + dot(table_low[...], high)
        result = result[:ROWS]
        full[...] = result
        to_y[...] = result[:, 384:512].astype(bf16)
        to_z[...] = jnp.where(y_hi == 0, result[:, 256:512], result[:, 0:256]).astype(bf16)


def cross(role, operands, before, tables, count):
    last = tables is not None
    start = before is None
    args = list(operands)
    in_specs = [pl.BlockSpec(memory_space=pl.ANY)] * len(operands)
    shape = (PAIRS, HALF, 2 * NF)
    tiles = HALF // TILE
    if not start:
        args.append(before)
        in_specs.append(pl.BlockSpec(shape, lambda i, role: (0, 0, 0)))
    scratch = [pltpu.VMEM((tiles, SLOTS, count, TILE, 2 * NF), bf16), pltpu.SemaphoreType.DMA((tiles, SLOTS))]
    if last:
        args += list(tables)
        in_specs += [pl.BlockSpec((TABLE_ROWS, 2 * NF), lambda i, role: (0, 0))] * 2
        out_shape = [
            jax.ShapeDtypeStruct((ROWS, PAIRS * HALF), f32),
            jax.ShapeDtypeStruct((ROWS, 128), bf16),
            jax.ShapeDtypeStruct((ROWS, 256), bf16),
        ]
        out_specs = [pl.BlockSpec(s.shape, lambda i, role: (0, 0)) for s in out_shape]
        scratch.append(pltpu.VMEM(shape, f32))
    else:
        out_shape = jax.ShapeDtypeStruct(shape, f32)
        out_specs = pl.BlockSpec(shape, lambda i, role: (0, 0, 0))
    return pl.pallas_call(
        functools.partial(cross_kernel, count, start, last),
        grid_spec=pltpu.PrefetchScalarGridSpec(
            num_scalar_prefetch=1, grid=(1,), in_specs=in_specs, out_specs=out_specs, scratch_shapes=scratch
        ),
        out_shape=out_shape,
        cost_estimate=pl.CostEstimate(
            flops=PAIRS * 8 * count * HALF * NF,
            bytes_accessed=SLOTS * count * HALF * 2 * NF * 2,
            transcendentals=0,
        ),
        name=f"cross_{'last' if last else 'first' if start else 'middle'}",
    )(role, *args)


def assemble_kernel(role, full, from_y, from_z, out):
    y_hi = role[0]
    core = role[1]
    a0 = (y_hi == 0) & (core == 0)
    a1 = (y_hi == 0) & (core != 0)
    b0 = (y_hi != 0) & (core == 0)
    is_a = y_hi == 0
    own = [full[:, i * HALF : (i + 1) * HALF] for i in range(PAIRS)]
    y0, y1 = [from_y[:, i * HALF : (i + 1) * HALF].astype(f32) for i in range(2)]
    z = [from_z[:, i * HALF : (i + 1) * HALF].astype(f32) for i in range(4)]
    p0, p1, p4, p5, q0, q1 = own[:6]

    def pick(for_a0, for_a1, for_b0, for_b1):
        return jnp.where(a0, for_a0, jnp.where(a1, for_a1, jnp.where(b0, for_b0, for_b1)))

    down = [pick(p5, p1, q1, y1), jnp.where(is_a, p0, y0), pick(p1, p5, y1, q1), jnp.where(is_a, p4, q0)]
    up = [pick(q1, y1, p5, z[1]), jnp.where(is_a, y0, z[0]), pick(y1, z[1], z[1], z[3]), jnp.where(is_a, z[0], z[2])]
    planes = [jnp.concatenate([d, u], axis=1) for d, u in zip(down, up)]
    for slot in range(REACH):
        distance = role[2 + slot]
        value = jnp.zeros((ROWS, 2 * HALF), f32)
        for k in range(REACH):
            value = jnp.where(distance == k + 1, planes[k], value)
        out[slot] = value.astype(bf16)


def assemble(role, full, from_y, from_z):
    return pl.pallas_call(
        assemble_kernel,
        grid_spec=pltpu.PrefetchScalarGridSpec(
            num_scalar_prefetch=1,
            grid=(1,),
            in_specs=[pl.BlockSpec(a.shape, lambda i, role: (0, 0)) for a in (full, from_y, from_z)],
            out_specs=pl.BlockSpec((REACH, ROWS, 2 * HALF), lambda i, role: (0, 0, 0)),
        ),
        out_shape=jax.ShapeDtypeStruct((REACH, ROWS, 2 * HALF), bf16),
        name="assemble",
    )(role, full, from_y, from_z)


def route(blocks, times, target):
    pairs = []
    for b in range(blocks):
        z, y_hi, core = b // 4, b // 2 % 2, b % 2
        for t in range(times):
            to_z, to_y, to_core, to_t = target(z, y_hi, core, t)
            if 0 <= to_z < blocks // 4:
                pairs.append((b * times + t, ((to_z * 2 + to_y) * 2 + to_core) * times + to_t))
    return pairs


def body(traces, valid_mask, pair_owner):
    blocks, times = lax.axis_size("chan"), lax.axis_size("tm")
    windows_all = traces.shape[1] * times

    def move(block, target):
        return lax.ppermute(block, ("chan", "tm"), route(blocks, times, target))

    def to_core(block):
        return move(block, lambda z, y, c, t: (z, y, 1 - c, t))

    def to_y(block):
        return move(block, lambda z, y, c, t: (z, 1 - y, c, t))

    reader = lax.axis_index("chan")
    places = jnp.arange(2 + REACH, dtype=jnp.int32)
    role = jnp.pad(pair_owner[0], (2, 0)) - reader
    role = jnp.where(places == 0, reader // 2 % 2, jnp.where(places == 1, reader % 2, role))
    forward, band = jnp.asarray(forward_table()), jnp.asarray(band_table())
    high, low = inverse_tables(windows_all)
    tables = (jnp.asarray(high), jnp.asarray(low))

    operands = []
    for first, count in CHUNKS:
        big, small, both = whiten(role, traces[0], valid_mask[0], forward, band, first, count)
        near_big = move(big, lambda z, y, c, t: (z - 1 + 2 * y, y, c, t))
        near_small = move(small, lambda z, y, c, t: (z + 1 - 2 * y, y, c, t))
        across = to_y(small)
        other_own = to_core(both)
        rest = (to_core(near_big), to_core(near_small), to_core(across))
        operands.append((big, small, other_own, near_big, near_small, across, *rest))
    stack = None
    for k, (first, count) in enumerate(CHUNKS):
        stack = cross(role, operands[k], stack, tables if k == len(CHUNKS) - 1 else None, count)
    full, for_y, for_z = stack
    from_y = to_y(for_y)
    from_z = move(for_z, lambda z, y, c, t: (z - 1, y, c, t))
    partial = assemble(role, full, from_y, from_z)
    for bit in (4, 1, 2):
        arrived = move(partial, lambda z, y, c, t: (z, y, c, t ^ bit))
        partial = partial.astype(f32) + arrived.astype(f32)
        if bit != 2:
            partial = partial.astype(bf16)
    return partial[None, :, :LAGS, :]


def solution(mesh):
    return jax.shard_map(
        body,
        mesh=mesh,
        in_specs=(P("chan", "tm", None, None), P("chan", "tm", None), P("chan", None)),
        out_specs=P("chan", None, None, None),
        check_vma=False,
    )
```

```python
import functools
import math

import jax
import jax.numpy as jnp
import numpy as np
from jax import lax
from jax.experimental import pallas as pl
from jax.experimental.pallas import tpu as pltpu
from jax.sharding import PartitionSpec as P

NF = 256
WIN = 1024
MAXLAG = 50
SMOOTH = 4
REACH = 4
LAGS = 2 * MAXLAG + 1
ROWS = 104
TABLE_ROWS = 112
HALF = 64
STEP = 3
TILE = 16
PLANES = 12
CHUNKS = ((0, 6), (6, 9), (15, 6), (21, 3))
GROUPS = ((0, 1), (2,), (3,))
VMEM = 24 << 20
WATER = 0.05
EPS = 1e-06


f32 = jnp.float32
bf16 = jnp.bfloat16


def forward_table():
    samples = np.arange(WIN, dtype=np.int32)
    bins = np.arange(1, NF + 1, dtype=np.int32)
    phase = samples[:, None] * bins[None, :] % WIN
    angle = phase.astype(np.float32) * np.float32(2.0 * math.pi / WIN)
    return np.concatenate([np.cos(angle), -np.sin(angle)], axis=1).astype(bf16)


def inverse_tables(windows_all):
    bins = np.arange(1, NF + 1, dtype=np.int32)
    offsets = np.arange(LAGS, dtype=np.int32) - MAXLAG
    phase = bins[None, :] * offsets[:, None] % WIN
    angle = phase.astype(np.float32) * np.float32(2.0 * math.pi / WIN)
    factor = np.float32(1.0 / math.sqrt(windows_all * NF))
    table = np.concatenate([np.cos(angle), -np.sin(angle)], axis=1) * factor
    table = np.pad(table, ((0, TABLE_ROWS - LAGS), (0, 0))).astype(np.float32)
    high = table.astype(bf16)
    low = (table - high.astype(np.float32)).astype(bf16)
    return high, low


def band_table():
    bins = np.arange(NF)
    near = np.abs(bins[:, None] - bins[None, :]) <= SMOOTH
    return np.concatenate([near, near], axis=0).astype(bf16)


def prepare(role, traces, mask, first, count):
    step = STEP
    base = first // step

    def kernel(role, traces, mask, out):
        i = pl.program_id(0)
        for j in range(step):
            keep = mask[pl.ds(first + i * step + j, 1), :].astype(f32).astype(bf16)
            out[j] = traces[j] * keep

    return pl.pallas_call(
        kernel,
        grid_spec=pltpu.PrefetchScalarGridSpec(
            num_scalar_prefetch=1,
            grid=(count // step,),
            in_specs=[
                pl.BlockSpec((step, HALF, WIN), lambda i, role: (base + i, 1 - role[1], 0)),
                pl.BlockSpec(mask.shape, lambda i, role: (0, 0)),
            ],
            out_specs=pl.BlockSpec((step, HALF, WIN), lambda i, role: (i, 0, 0)),
        ),
        out_shape=jax.ShapeDtypeStruct((count, HALF, WIN), bf16),
        compiler_params=pltpu.CompilerParams(vmem_limit_bytes=VMEM),
        cost_estimate=pl.CostEstimate(
            flops=count * HALF * WIN, bytes_accessed=4 * count * HALF * WIN, transcendentals=0
        ),
    )(role, traces, mask)


def whiten_kernel(first, role, traces, given, mask, forward, band, out, masked, spectra, split, level):
    step = pl.program_id(0)
    core = role[1]
    for j in range(STEP):
        keep = mask[pl.ds(first + step * STEP + j, 1), :].astype(f32).astype(bf16)
        masked[j * HALF : (j + 1) * HALF, :] = traces[j] * keep
        masked[(STEP + j) * HALF : (STEP + j + 1) * HALF, :] = given[j]
    spectra[...] = jnp.dot(masked[...], forward[...], preferred_element_type=f32)
    for r in range(0, 2 * STEP * HALF, 32):
        rows = slice(r, r + 32)
        real = spectra[rows, :NF]
        imag = spectra[rows, NF:]
        amplitude = jnp.sqrt(real * real + imag * imag)
        high = amplitude.astype(bf16)
        split[rows, :NF] = high
        split[rows, NF:] = (amplitude - high.astype(f32)).astype(bf16)
        total = jnp.sum(amplitude, axis=-1, keepdims=True)
        level[rows, :] = jnp.broadcast_to(total * f32(WATER / NF) + f32(EPS), (32, 128))
    smooth = jnp.dot(split[...], band[...], preferred_element_type=f32)
    for r in range(0, 2 * STEP * HALF, 32):
        rows = slice(r, r + 32)
        base = level[rows, :]
        divisor = smooth[rows, :] * f32(1.0 / (2 * SMOOTH + 1)) + jnp.concatenate([base, base], axis=1)
        inverse = 1.0 / divisor
        h, rest = divmod(r, STEP * HALF)
        j, c = divmod(rest, HALF)
        block = core if h == 0 else 1 - core
        out[block, j, c : c + 32, :NF] = (spectra[rows, :NF] * inverse).astype(bf16)
        out[block, j, c : c + 32, NF:] = (spectra[rows, NF:] * inverse).astype(bf16)


def whiten(role, traces, given, mask, forward, band, first, count, skip):
    rows = 2 * STEP * HALF
    base = first // STEP
    skip = skip // STEP
    return pl.pallas_call(
        functools.partial(whiten_kernel, first),
        grid_spec=pltpu.PrefetchScalarGridSpec(
            num_scalar_prefetch=1,
            grid=(count // STEP,),
            in_specs=[
                pl.BlockSpec((STEP, HALF, WIN), lambda i, role: (base + i, role[1], 0)),
                pl.BlockSpec((STEP, HALF, WIN), lambda i, role: (skip + i, 0, 0)),
                pl.BlockSpec(mask.shape, lambda i, role: (0, 0)),
                pl.BlockSpec(forward.shape, lambda i, role: (0, 0)),
                pl.BlockSpec(band.shape, lambda i, role: (0, 0)),
            ],
            out_specs=pl.BlockSpec((2, STEP, HALF, 2 * NF), lambda i, role: (0, i, 0, 0)),
            scratch_shapes=[
                pltpu.VMEM((rows, WIN), bf16),
                pltpu.VMEM((rows, 2 * NF), f32),
                pltpu.VMEM((rows, 2 * NF), bf16),
                pltpu.VMEM((rows, 128), f32),
            ],
        ),
        out_shape=jax.ShapeDtypeStruct((2, count, HALF, 2 * NF), bf16),
        compiler_params=pltpu.CompilerParams(vmem_limit_bytes=VMEM),
        cost_estimate=pl.CostEstimate(
            flops=2 * count * 2 * HALF * (WIN * 2 * NF + 2 * NF * NF),
            bytes_accessed=count * 2 * HALF * (WIN + 2 * NF) * 2,
            transcendentals=count * 2 * HALF * NF * 2,
        ),
    )(role, traces, given, mask, forward, band)


def cross_kernel(counts, start, last, role, *refs):
    sets = [refs[3 * k : 3 * k + 3] for k in range(len(counts))]
    refs = refs[3 * len(counts) :]
    before = None
    if not start:
        before, refs = refs[0], refs[1:]
    table_high, table_low, *refs = refs
    if last:
        kept, to_z, to_y, buf, sem, total = refs
    else:
        kept, buf, sem, total = refs
    y_hi = role[0]
    core = role[1]
    tiles = HALF // TILE
    offsets = [sum(counts[:k]) for k in range(len(counts))]

    def copy(source, k, t, slot):
        place = buf.at[t, pl.ds(slot, 2), pl.ds(offsets[k], counts[k])]
        return pltpu.make_async_copy(source.at[:, :, pl.ds(t * TILE, TILE), :], place, sem.at[k, t, slot // 2])

    for t in range(tiles):
        for k, (own, near, across) in enumerate(sets):
            copy(across, k, t, 4).start()

            @pl.when(core == 0)
            def _():
                copy(own, k, t, 0).start()
                copy(near, k, t, 2).start()

            @pl.when(core != 0)
            def _():
                copy(near, k, t, 0).start()
                copy(own, k, t, 2).start()

    count = sum(counts)
    zero = jnp.zeros((TILE, 128), f32)

    def tile(t, carry):
        for k in range(len(counts)):
            for slot in (0, 2, 4):
                copy(sets[k][2], k, t, slot).wait()
        rows = pl.ds(pl.multiple_of(t * TILE, TILE), TILE)
        for f in range(0, NF, 128):
            re = slice(f, f + 128)
            im = slice(NF + f, NF + f + 128)

            def run(pairs):
                slots = sorted({s for _, a, b in pairs for s in (a, b)})

                def window(w, sums):
                    at = {s: (buf[t, s, w, :, re].astype(f32), buf[t, s, w, :, im].astype(f32)) for s in slots}
                    out = []
                    for (_, a, b), (sr, si) in zip(pairs, sums):
                        ar, ai = at[a]
                        br, bi = at[b]
                        out.append((sr + (ar * br + ai * bi), si + (ar * bi - ai * br)))
                    return tuple(out)

                sums = lax.fori_loop(0, count, window, tuple((zero, zero) for _ in pairs), unroll=3)
                for (plane, _, _), (sr, si) in zip(pairs, sums):
                    total[plane, rows, re] = sr
                    total[plane, rows, im] = si

            inner = ((3, 0, 2), (6, 1, 2), (7, 1, 3))

            @pl.when(core == 0)
            def _():
                run(((0, 0, 1), *inner))

            @pl.when(core != 0)
            def _():
                run(((0, 2, 3), *inner))

            @pl.when(y_hi == core)
            def _():
                run(((1, 0, 4), (2, 0, 5), (4, 1, 4), (5, 1, 5)))
                run(((8, 4, 2), (9, 4, 3), (10, 5, 2), (11, 5, 3)))

            @pl.when(y_hi != core)
            def _():
                for plane in (1, 2, 4, 5, 8, 9, 10, 11):
                    total[plane, rows, re] = zero
                    total[plane, rows, im] = zero

        return carry

    lax.fori_loop(0, tiles, tile, 0)
    stack = total[...].reshape(PLANES * HALF, 2 * NF)
    high = stack.astype(bf16)
    low = (stack - high.astype(f32)).astype(bf16)
    dims = (((1,), (1,)), ((), ()))
    dot = functools.partial(lax.dot_general, dimension_numbers=dims, preferred_element_type=f32)
    result = dot(table_high[...], high) + dot(table_high[...], low) + dot(table_low[...], high)
    result = result[:ROWS]
    if not start:
        result = result + before[...]
    if not last:
        kept[...] = result
        return
    near_part = result[:, : 8 * HALF]
    lane = lax.broadcasted_iota(jnp.int32, near_part.shape, 1)
    local = lane < HALF
    kept[...] = jnp.where((lane < jnp.where(core == 0, 8 * HALF, HALF)), near_part, 0.0)
    to_z[...] = jnp.where(local, 0.0, near_part).astype(bf16)
    to_y[...] = result[:, 8 * HALF :].astype(bf16)


def whole(shape):
    return pl.BlockSpec(shape, lambda i, role: (0,) * len(shape))


def cross(role, sets, before, tables, last):
    counts = tuple(s[0].shape[1] for s in sets)
    start = before is None
    args = [a for s in sets for a in s]
    in_specs = [pl.BlockSpec(memory_space=pl.ANY)] * len(args)
    if not start:
        args.append(before)
        in_specs.append(whole(before.shape))
    args += list(tables)
    in_specs += [whole((TABLE_ROWS, 2 * NF))] * 2
    tiles = HALF // TILE
    scratch = [
        pltpu.VMEM((tiles, 6, sum(counts), TILE, 2 * NF), bf16),
        pltpu.SemaphoreType.DMA((len(counts), tiles, 3)),
        pltpu.VMEM((PLANES, HALF, 2 * NF), f32),
    ]
    if last:
        out_shape = [
            jax.ShapeDtypeStruct((ROWS, 8 * HALF), f32),
            jax.ShapeDtypeStruct((ROWS, 8 * HALF), bf16),
            jax.ShapeDtypeStruct((ROWS, 4 * HALF), bf16),
        ]
        out_specs = [whole(s.shape) for s in out_shape]
    else:
        out_shape = jax.ShapeDtypeStruct((ROWS, PLANES * HALF), f32)
        out_specs = whole(out_shape.shape)
    return pl.pallas_call(
        functools.partial(cross_kernel, counts, start, last),
        grid_spec=pltpu.PrefetchScalarGridSpec(
            num_scalar_prefetch=1, grid=(1,), in_specs=in_specs, out_specs=out_specs, scratch_shapes=scratch
        ),
        out_shape=out_shape,
        compiler_params=pltpu.CompilerParams(vmem_limit_bytes=VMEM),
        cost_estimate=pl.CostEstimate(
            flops=PLANES * 8 * sum(counts) * HALF * NF,
            bytes_accessed=6 * sum(counts) * HALF * 2 * NF * 2,
            transcendentals=0,
        ),
        name="cross_last" if last else "cross_first" if start else "cross_middle",
    )(role, *args)


def combine_kernel(role, kept, from_z, from_y, own, give):
    core = role[1]
    y = from_y[...].astype(f32)
    gap = jnp.zeros((ROWS, HALF), f32)
    placed = jnp.concatenate([gap, y[:, : 2 * HALF], gap, y[:, 2 * HALF :], gap, gap], axis=1)
    total = (kept[...] + from_z[...].astype(f32) + placed).astype(bf16)
    first, second = total[:, : 4 * HALF].astype(f32), total[:, 4 * HALF :].astype(f32)
    own[...] = jnp.where(core == 0, first, second).astype(bf16)
    give[...] = jnp.where(core == 0, second, first).astype(bf16)


def combine(role, kept, from_z, from_y):
    part = jax.ShapeDtypeStruct((ROWS, 4 * HALF), bf16)
    return pl.pallas_call(
        combine_kernel,
        grid_spec=pltpu.PrefetchScalarGridSpec(
            num_scalar_prefetch=1,
            grid=(1,),
            in_specs=[whole(a.shape) for a in (kept, from_z, from_y)],
            out_specs=[whole(part.shape)] * 2,
        ),
        out_shape=[part, part],
        compiler_params=pltpu.CompilerParams(vmem_limit_bytes=VMEM),
        name="combine",
    )(role, kept, from_z, from_y)


def assemble_kernel(role, slots, own, got, out):
    core = role[1]
    mine, other = own[...].astype(f32), got[...].astype(f32)
    first = jnp.where(core == 0, mine, other)
    second = jnp.where(core == 0, other, mine)
    planes = [
        jnp.concatenate([first[:, i * HALF : (i + 1) * HALF], second[:, i * HALF : (i + 1) * HALF]], axis=1)
        for i in range(REACH)
    ]
    for slot in range(REACH):
        distance = slots[slot]
        value = jnp.zeros((ROWS, 2 * HALF), f32)
        for k in range(REACH):
            value = jnp.where(distance == k + 1, planes[k], value)
        out[:, slot * 2 * HALF : (slot + 1) * 2 * HALF] = value.astype(bf16)


def assemble(role, slots, own, got):
    shape = (ROWS, REACH * 2 * HALF)
    return pl.pallas_call(
        assemble_kernel,
        grid_spec=pltpu.PrefetchScalarGridSpec(
            num_scalar_prefetch=2,
            grid=(1,),
            in_specs=[pl.BlockSpec(own.shape, lambda i, *_: (0, 0)), pl.BlockSpec(got.shape, lambda i, *_: (0, 0))],
            out_specs=pl.BlockSpec(shape, lambda i, *_: (0, 0)),
        ),
        out_shape=jax.ShapeDtypeStruct(shape, bf16),
        compiler_params=pltpu.CompilerParams(vmem_limit_bytes=VMEM),
        name="assemble",
    )(role, slots, own, got)


def route(blocks, times, target):
    pairs = []
    for b in range(blocks):
        z, y_hi, core = b // 4, b // 2 % 2, b % 2
        for t in range(times):
            to_z, to_y, to_core, to_t = target(z, y_hi, core, t)
            if 0 <= to_z < blocks // 4:
                pairs.append((b * times + t, ((to_z * 2 + to_y) * 2 + to_core) * times + to_t))
    return pairs


def body(traces, valid_mask, pair_owner):
    blocks, times = lax.axis_size("chan"), lax.axis_size("tm")
    windows_all = traces.shape[1] * times

    def move(block, target):
        return lax.ppermute(block, ("chan", "tm"), route(blocks, times, target))

    def to_core(block):
        return move(block, lambda z, y, c, t: (z, y, 1 - c, t))

    reader = lax.axis_index("chan")
    core = reader % 2
    role = jnp.where(jnp.arange(2, dtype=jnp.int32) == 0, reader // 2 % 2, core)
    slots = pair_owner[0] - reader
    forward, band = jnp.asarray(forward_table()), jnp.asarray(band_table())
    high, low = inverse_tables(windows_all)
    tables = (jnp.asarray(high), jnp.asarray(low))
    mask = valid_mask[0]

    rest = CHUNKS[0][1]
    later = traces.shape[1] - rest
    head = prepare(role, traces[0], mask, 0, rest)
    head = to_core(head)
    body_part = prepare(role, traces[0], mask, rest, later)
    body_part = to_core(body_part)
    sets = []
    order = role
    for k, (first, count) in enumerate(CHUNKS):
        given, skip = (head, 0) if k == 0 else (body_part, first - rest)
        own = whiten(order, traces[0], given, mask, forward, band, first, count, skip)
        own, order = lax.optimization_barrier((own, order))
        near = move(own, lambda z, y, c, t: (z - 1 + 2 * c, y, c, t))
        across = move(own, lambda z, y, c, t: (z, 1 - y, c, t) if y != c else (-1, y, c, t))
        sets.append((own, near, across))
    stack = None
    for k, group in enumerate(GROUPS):
        stack = cross(order, [sets[i] for i in group], stack, tables, k == len(GROUPS) - 1)
    kept, for_z, for_y = stack
    from_z = move(for_z, lambda z, y, c, t: (z - 1 if c else -1, y, c, t))
    from_y = move(for_y, lambda z, y, c, t: (z if y == c else -1, 1 - y, c, t))
    mine, give = combine(role, kept, from_z, from_y)
    partial = assemble(role, slots, mine, to_core(give))
    for bit in (4, 1, 2):
        arrived = move(partial, lambda z, y, c, t: (z, y, c, t ^ bit))
        partial = partial.astype(f32) + arrived.astype(f32)
        if bit != 2:
            partial = partial.astype(bf16)
    result = partial[:LAGS].reshape(LAGS, REACH, 2 * HALF)
    return result.transpose(1, 0, 2)[None]


def solution(mesh):
    return jax.shard_map(
        body,
        mesh=mesh,
        in_specs=(P("chan", "tm", None, None), P("chan", "tm", None), P("chan", None)),
        out_specs=P("chan", None, None, None),
        check_vma=False,
    )
```

```python
import functools
import math

import jax
import jax.numpy as jnp
import numpy as np
from jax import lax
from jax.experimental import pallas as pl
from jax.experimental.pallas import tpu as pltpu
from jax.sharding import PartitionSpec as P

NF = 256
WIN = 1024
MAXLAG = 50
SMOOTH = 4
REACH = 4
LAGS = 2 * MAXLAG + 1
ROWS = 104
TABLE_ROWS = 112
HALF = 64
STEP = 3
TILE = 16
PLANES = 12
CHUNKS = ((0, 6), (6, 9), (15, 6), (21, 3))
VMEM = 24 << 20
WATER = 0.05
EPS = 1e-06


f32 = jnp.float32
bf16 = jnp.bfloat16


def forward_table():
    samples = np.arange(WIN, dtype=np.int32)
    bins = np.arange(1, NF + 1, dtype=np.int32)
    phase = samples[:, None] * bins[None, :] % WIN
    angle = phase.astype(np.float32) * np.float32(2.0 * math.pi / WIN)
    return np.concatenate([np.cos(angle), -np.sin(angle)], axis=1).astype(bf16)


def inverse_tables(windows_all):
    bins = np.arange(1, NF + 1, dtype=np.int32)
    offsets = np.arange(LAGS, dtype=np.int32) - MAXLAG
    phase = bins[None, :] * offsets[:, None] % WIN
    angle = phase.astype(np.float32) * np.float32(2.0 * math.pi / WIN)
    factor = np.float32(1.0 / math.sqrt(windows_all * NF))
    table = np.concatenate([np.cos(angle), -np.sin(angle)], axis=1) * factor
    table = np.pad(table, ((0, TABLE_ROWS - LAGS), (0, 0))).astype(np.float32)
    high = table.astype(bf16)
    low = (table - high.astype(np.float32)).astype(bf16)
    return high, low


def band_table():
    bins = np.arange(NF)
    near = np.abs(bins[:, None] - bins[None, :]) <= SMOOTH
    return np.concatenate([near, near], axis=0).astype(bf16)


def prepare_kernel(first, role, traces, mask, own, give):
    i = pl.program_id(0)
    core = role[1]
    for j in range(STEP):
        keep = mask[pl.ds(first + i * STEP + j, 1), :].astype(bf16)
        own[j] = traces[j, pl.ds(pl.multiple_of(core * HALF, HALF), HALF), :] * keep
        give[j] = traces[j, pl.ds(pl.multiple_of((1 - core) * HALF, HALF), HALF), :] * keep


def prepare(role, traces, mask, first, count):
    base = first // STEP
    block = pl.BlockSpec((STEP, HALF, WIN), lambda i, role: (i, 0, 0))
    part = jax.ShapeDtypeStruct((count, HALF, WIN), bf16)
    return pl.pallas_call(
        functools.partial(prepare_kernel, first),
        grid_spec=pltpu.PrefetchScalarGridSpec(
            num_scalar_prefetch=1,
            grid=(count // STEP,),
            in_specs=[
                pl.BlockSpec((STEP, 2 * HALF, WIN), lambda i, role: (base + i, 0, 0)),
                pl.BlockSpec(mask.shape, lambda i, role: (0, 0)),
            ],
            out_specs=[block, block],
        ),
        out_shape=[part, part],
        compiler_params=pltpu.CompilerParams(vmem_limit_bytes=VMEM),
        cost_estimate=pl.CostEstimate(
            flops=2 * count * HALF * WIN, bytes_accessed=8 * count * HALF * WIN, transcendentals=0
        ),
    )(role, traces, mask)


def whiten_kernel(role, kept, given, forward, band, out, spectra, split, level):
    core = role[1]
    part = STEP * HALF
    spectra[:part] = jnp.dot(kept[...].reshape(part, WIN), forward[...], preferred_element_type=f32)
    spectra[part:] = jnp.dot(given[...].reshape(part, WIN), forward[...], preferred_element_type=f32)
    for r in range(0, 2 * STEP * HALF, 32):
        rows = slice(r, r + 32)
        real = spectra[rows, :NF]
        imag = spectra[rows, NF:]
        amplitude = jnp.sqrt(real * real + imag * imag)
        high = amplitude.astype(bf16)
        split[rows, :NF] = high
        split[rows, NF:] = (amplitude - high.astype(f32)).astype(bf16)
        total = jnp.sum(amplitude, axis=-1, keepdims=True)
        level[rows, :] = jnp.broadcast_to(total * f32(WATER / NF) + f32(EPS), (32, 128))
    smooth = jnp.dot(split[...], band[...], preferred_element_type=f32)
    for r in range(0, 2 * STEP * HALF, 32):
        rows = slice(r, r + 32)
        base = level[rows, :]
        divisor = smooth[rows, :] * f32(1.0 / (2 * SMOOTH + 1)) + jnp.concatenate([base, base], axis=1)
        inverse = 1.0 / divisor
        h, rest = divmod(r, STEP * HALF)
        j, c = divmod(rest, HALF)
        block = core if h == 0 else 1 - core
        out[block, j, c : c + 32, :NF] = (spectra[rows, :NF] * inverse).astype(bf16)
        out[block, j, c : c + 32, NF:] = (spectra[rows, NF:] * inverse).astype(bf16)


def whiten(role, kept, given, forward, band, count, skip):
    rows = 2 * STEP * HALF
    skip = skip // STEP
    return pl.pallas_call(
        whiten_kernel,
        grid_spec=pltpu.PrefetchScalarGridSpec(
            num_scalar_prefetch=1,
            grid=(count // STEP,),
            in_specs=[
                pl.BlockSpec((STEP, HALF, WIN), lambda i, role: (skip + i, 0, 0)),
                pl.BlockSpec((STEP, HALF, WIN), lambda i, role: (skip + i, 0, 0)),
                pl.BlockSpec(forward.shape, lambda i, role: (0, 0)),
                pl.BlockSpec(band.shape, lambda i, role: (0, 0)),
            ],
            out_specs=pl.BlockSpec((2, STEP, HALF, 2 * NF), lambda i, role: (0, i, 0, 0)),
            scratch_shapes=[
                pltpu.VMEM((rows, 2 * NF), f32),
                pltpu.VMEM((rows, 2 * NF), bf16),
                pltpu.VMEM((rows, 128), f32),
            ],
        ),
        out_shape=jax.ShapeDtypeStruct((2, count, HALF, 2 * NF), bf16),
        compiler_params=pltpu.CompilerParams(vmem_limit_bytes=VMEM),
        cost_estimate=pl.CostEstimate(
            flops=2 * count * 2 * HALF * (WIN * 2 * NF + 2 * NF * NF),
            bytes_accessed=count * 2 * HALF * (WIN + 2 * NF) * 2,
            transcendentals=count * 2 * HALF * NF * 2,
        ),
    )(role, kept, given, forward, band)


def cross_kernel(start, last, role, own, near, across, *refs):
    before = None
    if not start:
        before, refs = refs[0], refs[1:]
    table_high, table_low, *refs = refs
    if last:
        kept, to_z, to_y, total = refs
    else:
        kept, total = refs
    y_hi = role[0]
    core = role[1]
    count = own.shape[1]
    zero = jnp.zeros((TILE, 128), f32)

    def tile(t, carry):
        rows = pl.ds(pl.multiple_of(t * TILE, TILE), TILE)
        for f in range(0, NF, 128):
            re = slice(f, f + 128)
            im = slice(NF + f, NF + f + 128)

            def run(blocks, pairs):
                used = sorted({s for _, a, b in pairs for s in (a, b)})

                def window(w, sums):
                    at = {}
                    for s in used:
                        ref = blocks[s // 2]
                        at[s] = (ref[s % 2, w, rows, re].astype(f32), ref[s % 2, w, rows, im].astype(f32))
                    out = []
                    for (_, a, b), (sr, si) in zip(pairs, sums):
                        ar, ai = at[a]
                        br, bi = at[b]
                        out.append((sr + (ar * br + ai * bi), si + (ar * bi - ai * br)))
                    return tuple(out)

                sums = lax.fori_loop(0, count, window, tuple((zero, zero) for _ in pairs), unroll=3)
                for (plane, _, _), (sr, si) in zip(pairs, sums):
                    total[plane, rows, re] = sr
                    total[plane, rows, im] = si

            inner = ((3, 0, 2), (6, 1, 2), (7, 1, 3))

            def all_pairs(blocks, local):
                run(blocks, (local, *inner))

                @pl.when(y_hi == core)
                def _():
                    run(blocks, ((1, 0, 4), (2, 0, 5), (4, 1, 4), (5, 1, 5)))
                    run(blocks, ((8, 4, 2), (9, 4, 3), (10, 5, 2), (11, 5, 3)))

            @pl.when(core == 0)
            def _():
                all_pairs((own, near, across), (0, 0, 1))

            @pl.when(core != 0)
            def _():
                all_pairs((near, own, across), (0, 2, 3))

            @pl.when(y_hi != core)
            def _():
                for plane in (1, 2, 4, 5, 8, 9, 10, 11):
                    total[plane, rows, re] = zero
                    total[plane, rows, im] = zero

        return carry

    lax.fori_loop(0, HALF // TILE, tile, 0)
    stack = total[...].reshape(PLANES * HALF, 2 * NF)
    high = stack.astype(bf16)
    dims = (((1,), (1,)), ((), ()))
    dot = functools.partial(lax.dot_general, dimension_numbers=dims, preferred_element_type=f32)
    result = dot(table_high[...], high)
    if not last:
        low = (stack - high.astype(f32)).astype(bf16)
        result = result + (dot(table_high[...], low) + dot(table_low[...], high))
    result = result[:ROWS]
    if not start:
        result = result + before[...]
    if not last:
        kept[...] = result
        return
    near_part = result[:, : 8 * HALF]
    lane = lax.broadcasted_iota(jnp.int32, near_part.shape, 1)
    kept[...] = jnp.where((lane < jnp.where(core == 0, 8 * HALF, HALF)), near_part, 0.0)
    to_z[...] = jnp.where(lane < HALF, 0.0, near_part).astype(bf16)
    to_y[...] = result[:, 8 * HALF :].astype(bf16)


def whole(shape):
    return pl.BlockSpec(shape, lambda i, role: (0,) * len(shape))


def cross(role, operands, before, tables, last):
    start = before is None
    count = operands[0].shape[1]
    args = [role, *operands]
    if not start:
        args.append(before)
    args += list(tables)
    in_vmem = pl.BlockSpec(memory_space=pltpu.VMEM)
    if last:
        out_shape = [
            jax.ShapeDtypeStruct((ROWS, 8 * HALF), f32),
            jax.ShapeDtypeStruct((ROWS, 8 * HALF), bf16),
            jax.ShapeDtypeStruct((ROWS, 4 * HALF), bf16),
        ]
        out_specs = [in_vmem] * 3
    else:
        out_shape = jax.ShapeDtypeStruct((ROWS, PLANES * HALF), f32)
        out_specs = in_vmem
    return pl.pallas_call(
        functools.partial(cross_kernel, start, last),
        in_specs=[pl.BlockSpec(memory_space=pltpu.SMEM)] + [in_vmem] * (len(args) - 1),
        out_specs=out_specs,
        out_shape=out_shape,
        scratch_shapes=[pltpu.VMEM((PLANES, HALF, 2 * NF), f32)],
        compiler_params=pltpu.CompilerParams(vmem_limit_bytes=VMEM),
        cost_estimate=pl.CostEstimate(
            flops=PLANES * 8 * count * HALF * NF,
            bytes_accessed=6 * count * HALF * 2 * NF * 2,
            transcendentals=0,
        ),
    )(*args)


def combine_kernel(role, kept, from_z, from_y, own, give):
    core = role[1]
    y = jnp.where(role[0] != core, from_y[...].astype(f32), 0.0)
    z = jnp.where((core != 0) & (role[2] == 0), from_z[...].astype(f32), 0.0)
    gap = jnp.zeros((ROWS, HALF), f32)
    placed = jnp.concatenate([gap, y[:, : 2 * HALF], gap, y[:, 2 * HALF :], gap, gap], axis=1)
    total = (kept[...] + z + placed).astype(bf16)
    first, second = total[:, : 4 * HALF].astype(f32), total[:, 4 * HALF :].astype(f32)
    own[...] = jnp.where(core == 0, first, second).astype(bf16)
    give[...] = jnp.where(core == 0, second, first).astype(bf16)


def combine(role, kept, from_z, from_y):
    part = jax.ShapeDtypeStruct((ROWS, 4 * HALF), bf16)
    return pl.pallas_call(
        combine_kernel,
        grid_spec=pltpu.PrefetchScalarGridSpec(
            num_scalar_prefetch=1,
            grid=(1,),
            in_specs=[whole(a.shape) for a in (kept, from_z, from_y)],
            out_specs=[whole(part.shape)] * 2,
        ),
        out_shape=[part, part],
        compiler_params=pltpu.CompilerParams(vmem_limit_bytes=VMEM),
        name="combine",
    )(role, kept, from_z, from_y)


def assemble_kernel(role, slots, own, got, out):
    core = role[1]
    mine, other = own[...].astype(f32), got[...].astype(f32)
    first = jnp.where(core == 0, mine, other)
    second = jnp.where(core == 0, other, mine)
    planes = [
        jnp.concatenate([first[:, i * HALF : (i + 1) * HALF], second[:, i * HALF : (i + 1) * HALF]], axis=1)
        for i in range(REACH)
    ]
    for slot in range(REACH):
        distance = slots[slot]
        value = jnp.zeros((ROWS, 2 * HALF), f32)
        for k in range(REACH):
            value = jnp.where(distance == k + 1, planes[k], value)
        out[:, slot * 2 * HALF : (slot + 1) * 2 * HALF] = value.astype(bf16)


def assemble(role, slots, own, got):
    shape = (ROWS, REACH * 2 * HALF)
    return pl.pallas_call(
        assemble_kernel,
        grid_spec=pltpu.PrefetchScalarGridSpec(
            num_scalar_prefetch=2,
            grid=(1,),
            in_specs=[pl.BlockSpec(own.shape, lambda i, *_: (0, 0)), pl.BlockSpec(got.shape, lambda i, *_: (0, 0))],
            out_specs=pl.BlockSpec(shape, lambda i, *_: (0, 0)),
        ),
        out_shape=jax.ShapeDtypeStruct(shape, bf16),
        compiler_params=pltpu.CompilerParams(vmem_limit_bytes=VMEM),
        name="assemble",
    )(role, slots, own, got)


def route(blocks, times, target):
    pairs = []
    for b in range(blocks):
        z, y_hi, core = b // 4, b // 2 % 2, b % 2
        for t in range(times):
            to_z, to_y, to_core, to_t = target(z, y_hi, core, t)
            if not 0 <= to_z < blocks // 4:
                to_z, to_core = z, 1 - core
            pairs.append((b * times + t, ((to_z * 2 + to_y) * 2 + to_core) * times + to_t))
    return pairs


def body(traces, valid_mask, pair_owner):
    blocks, times = lax.axis_size("chan"), lax.axis_size("tm")
    windows_all = traces.shape[1] * times

    def move(block, target):
        return lax.ppermute(block, ("chan", "tm"), route(blocks, times, target))

    def to_core(block):
        return move(block, lambda z, y, c, t: (z, y, 1 - c, t))

    reader = lax.axis_index("chan")
    core = reader % 2
    top = (reader // 4 == blocks // 4 - 1).astype(jnp.int32)
    places = jnp.arange(3, dtype=jnp.int32)
    role = jnp.where(places == 0, reader // 2 % 2, jnp.where(places == 1, core, top))
    slots = pair_owner[0] - reader
    forward, band = jnp.asarray(forward_table()), jnp.asarray(band_table())
    high, low = inverse_tables(windows_all)
    tables = (jnp.asarray(high), jnp.asarray(low))
    mask = valid_mask[0].astype(f32)

    rest = CHUNKS[0][1]
    later = traces.shape[1] - rest
    head, give = prepare(role, traces[0], mask, 0, rest)
    given_head = to_core(give)
    tail, give = prepare(role, traces[0], mask, rest, later)
    given_tail = to_core(give)
    sets = []
    order = role
    for k, (first, count) in enumerate(CHUNKS):
        if k == 0:
            own = whiten(order, head, given_head, forward, band, count, 0)
        else:
            own = whiten(order, tail, given_tail, forward, band, count, first - rest)
        own, order = lax.optimization_barrier((own, order))
        near = move(own, lambda z, y, c, t: (z - 1 + 2 * c, y, c, t))
        across = move(own, lambda z, y, c, t: (z, 1 - y, c, t) if y != c else (z, y, 1 - c, t))
        sets.append((own, near, across))
    stack = None
    for k, operands in enumerate(sets):
        stack = cross(order, operands, stack, tables, k == len(sets) - 1)
    kept, for_z, for_y = stack
    from_z = move(for_z, lambda z, y, c, t: (z + 1 - 2 * c, y, c, t))
    from_y = move(for_y, lambda z, y, c, t: (z, 1 - y, c, t) if y == c else (z, y, 1 - c, t))
    mine, give = combine(role, kept, from_z, from_y)
    partial = assemble(role, slots, mine, to_core(give))

    def exchange(block, bit):
        return move(block, lambda z, y, c, t: (z, y, c, t ^ bit)).astype(f32)

    partial = (partial.astype(f32) + exchange(partial, 4)).astype(bf16)
    far, third, near = (exchange(partial, bit) for bit in (2, 3, 1))
    partial = (partial.astype(f32) + near) + (far + third)
    result = partial[:LAGS].reshape(LAGS, REACH, 2 * HALF)
    return result.transpose(1, 0, 2)[None]


def solution(mesh):
    return jax.shard_map(
        body,
        mesh=mesh,
        in_specs=(P("chan", "tm", None, None), P("chan", "tm", None), P("chan", None)),
        out_specs=P("chan", None, None, None),
        check_vma=False,
    )
```

```python
import functools
import math

import jax
import jax.numpy as jnp
import numpy as np
from jax import lax
from jax.experimental import pallas as pl
from jax.experimental.pallas import tpu as pltpu
from jax.sharding import PartitionSpec as P

NF = 256
WIN = 1024
MAXLAG = 50
SMOOTH = 4
REACH = 4
LAGS = 2 * MAXLAG + 1
ROWS = 104
TABLE_ROWS = 112
HALF = 64
STEP = 3
TILE = 16
PLANES = 12
CHUNKS = ((0, 6), (6, 12), (18, 3), (21, 3))
VMEM = 24 << 20
WATER = 0.05
EPS = 1e-06


f32 = jnp.float32
bf16 = jnp.bfloat16


def forward_table():
    samples = np.arange(WIN, dtype=np.int32)
    bins = np.arange(1, NF + 1, dtype=np.int32)
    phase = samples[:, None] * bins[None, :] % WIN
    angle = phase.astype(np.float32) * np.float32(2.0 * math.pi / WIN)
    return np.concatenate([np.cos(angle), -np.sin(angle)], axis=1).astype(bf16)


def inverse_tables(windows_all):
    bins = np.arange(1, NF + 1, dtype=np.int32)
    offsets = np.arange(LAGS, dtype=np.int32) - MAXLAG
    phase = bins[None, :] * offsets[:, None] % WIN
    angle = phase.astype(np.float32) * np.float32(2.0 * math.pi / WIN)
    factor = np.float32(1.0 / math.sqrt(windows_all * NF))
    table = np.concatenate([np.cos(angle), -np.sin(angle)], axis=1) * factor
    table = np.pad(table, ((0, TABLE_ROWS - LAGS), (0, 0))).astype(np.float32)
    high = table.astype(bf16)
    low = (table - high.astype(np.float32)).astype(bf16)
    return high, low


def band_table():
    bins = np.arange(NF)
    near = np.abs(bins[:, None] - bins[None, :]) <= SMOOTH
    return np.concatenate([near, near], axis=0).astype(bf16)


def prepare_kernel(first, role, traces, mask, own, give):
    i = pl.program_id(0)
    core = role[1]
    for j in range(STEP):
        keep = mask[pl.ds(first + i * STEP + j, 1), :].astype(f32).astype(bf16)
        own[j] = traces[j, pl.ds(pl.multiple_of(core * HALF, HALF), HALF), :] * keep
        give[j] = traces[j, pl.ds(pl.multiple_of((1 - core) * HALF, HALF), HALF), :] * keep


def prepare(role, traces, mask, first, count):
    base = first // STEP
    block = pl.BlockSpec((STEP, HALF, WIN), lambda i, role: (i, 0, 0))
    part = jax.ShapeDtypeStruct((count, HALF, WIN), bf16)
    return pl.pallas_call(
        functools.partial(prepare_kernel, first),
        grid_spec=pltpu.PrefetchScalarGridSpec(
            num_scalar_prefetch=1,
            grid=(count // STEP,),
            in_specs=[
                pl.BlockSpec((STEP, 2 * HALF, WIN), lambda i, role: (base + i, 0, 0)),
                pl.BlockSpec(mask.shape, lambda i, role: (0, 0)),
            ],
            out_specs=[block, block],
        ),
        out_shape=[part, part],
        compiler_params=pltpu.CompilerParams(vmem_limit_bytes=VMEM),
        cost_estimate=pl.CostEstimate(
            flops=2 * count * HALF * WIN, bytes_accessed=8 * count * HALF * WIN, transcendentals=0
        ),
    )(role, traces, mask)


def whiten_kernel(role, kept, given, forward, band, out, spectra, split, level):
    core = role[1]
    part = STEP * HALF
    spectra[:part] = jnp.dot(kept[...].reshape(part, WIN), forward[...], preferred_element_type=f32)
    spectra[part:] = jnp.dot(given[...].reshape(part, WIN), forward[...], preferred_element_type=f32)
    for r in range(0, 2 * STEP * HALF, 32):
        rows = slice(r, r + 32)
        real = spectra[rows, :NF]
        imag = spectra[rows, NF:]
        amplitude = jnp.sqrt(real * real + imag * imag)
        high = amplitude.astype(bf16)
        split[rows, :NF] = high
        split[rows, NF:] = (amplitude - high.astype(f32)).astype(bf16)
        total = jnp.sum(amplitude, axis=-1, keepdims=True)
        level[rows, :] = jnp.broadcast_to(total * f32(WATER / NF) + f32(EPS), (32, 128))
    smooth = jnp.dot(split[...], band[...], preferred_element_type=f32)
    for r in range(0, 2 * STEP * HALF, 32):
        rows = slice(r, r + 32)
        base = level[rows, :]
        divisor = smooth[rows, :] * f32(1.0 / (2 * SMOOTH + 1)) + jnp.concatenate([base, base], axis=1)
        inverse = 1.0 / divisor
        h, rest = divmod(r, STEP * HALF)
        j, c = divmod(rest, HALF)
        block = core if h == 0 else 1 - core
        out[block, j, c : c + 32, :NF] = (spectra[rows, :NF] * inverse).astype(bf16)
        out[block, j, c : c + 32, NF:] = (spectra[rows, NF:] * inverse).astype(bf16)


def whiten(role, kept, given, forward, band, count, skip):
    rows = 2 * STEP * HALF
    skip = skip // STEP
    return pl.pallas_call(
        whiten_kernel,
        grid_spec=pltpu.PrefetchScalarGridSpec(
            num_scalar_prefetch=1,
            grid=(count // STEP,),
            in_specs=[
                pl.BlockSpec((STEP, HALF, WIN), lambda i, role: (skip + i, 0, 0)),
                pl.BlockSpec((STEP, HALF, WIN), lambda i, role: (skip + i, 0, 0)),
                pl.BlockSpec(forward.shape, lambda i, role: (0, 0)),
                pl.BlockSpec(band.shape, lambda i, role: (0, 0)),
            ],
            out_specs=pl.BlockSpec((2, STEP, HALF, 2 * NF), lambda i, role: (0, i, 0, 0)),
            scratch_shapes=[
                pltpu.VMEM((rows, 2 * NF), f32),
                pltpu.VMEM((rows, 2 * NF), bf16),
                pltpu.VMEM((rows, 128), f32),
            ],
        ),
        out_shape=jax.ShapeDtypeStruct((2, count, HALF, 2 * NF), bf16),
        compiler_params=pltpu.CompilerParams(vmem_limit_bytes=VMEM),
        cost_estimate=pl.CostEstimate(
            flops=2 * count * 2 * HALF * (WIN * 2 * NF + 2 * NF * NF),
            bytes_accessed=count * 2 * HALF * (WIN + 2 * NF) * 2,
            transcendentals=count * 2 * HALF * NF * 2,
        ),
    )(role, kept, given, forward, band)


def cross_kernel(start, last, role, own, near, across, *refs):
    before = None
    if not start:
        before, refs = refs[0], refs[1:]
    table_high, table_low, *refs = refs
    if last:
        kept, to_z, to_y, total = refs
    else:
        kept, total = refs
    y_hi = role[0]
    core = role[1]
    count = own.shape[1]
    zero = jnp.zeros((TILE, 128), f32)

    def tile(t, carry):
        rows = pl.ds(pl.multiple_of(t * TILE, TILE), TILE)
        for f in range(0, NF, 128):
            re = slice(f, f + 128)
            im = slice(NF + f, NF + f + 128)

            def run(blocks, pairs):
                used = sorted({s for _, a, b in pairs for s in (a, b)})

                def window(w, sums):
                    at = {}
                    for s in used:
                        ref = blocks[s // 2]
                        at[s] = (ref[s % 2, w, rows, re].astype(f32), ref[s % 2, w, rows, im].astype(f32))
                    out = []
                    for (_, a, b), (sr, si) in zip(pairs, sums):
                        ar, ai = at[a]
                        br, bi = at[b]
                        out.append((sr + (ar * br + ai * bi), si + (ar * bi - ai * br)))
                    return tuple(out)

                sums = lax.fori_loop(0, count, window, tuple((zero, zero) for _ in pairs), unroll=3)
                for (plane, _, _), (sr, si) in zip(pairs, sums):
                    total[plane, rows, re] = sr
                    total[plane, rows, im] = si

            inner = ((3, 0, 2), (6, 1, 2), (7, 1, 3))

            def all_pairs(blocks, local):
                run(blocks, (local, *inner))

                @pl.when(y_hi == core)
                def _():
                    run(blocks, ((1, 0, 4), (2, 0, 5), (4, 1, 4), (5, 1, 5)))
                    run(blocks, ((8, 4, 2), (9, 4, 3), (10, 5, 2), (11, 5, 3)))

            @pl.when(core == 0)
            def _():
                all_pairs((own, near, across), (0, 0, 1))

            @pl.when(core != 0)
            def _():
                all_pairs((near, own, across), (0, 2, 3))

            @pl.when(y_hi != core)
            def _():
                for plane in (1, 2, 4, 5, 8, 9, 10, 11):
                    total[plane, rows, re] = zero
                    total[plane, rows, im] = zero

        return carry

    lax.fori_loop(0, HALF // TILE, tile, 0)
    stack = total[...].reshape(PLANES * HALF, 2 * NF)
    high = stack.astype(bf16)
    dims = (((1,), (1,)), ((), ()))
    dot = functools.partial(lax.dot_general, dimension_numbers=dims, preferred_element_type=f32)
    result = dot(table_high[...], high)
    if not last:
        low = (stack - high.astype(f32)).astype(bf16)
        result = result + (dot(table_high[...], low) + dot(table_low[...], high))
    result = result[:ROWS]
    if not start:
        result = result + before[...]
    if not last:
        kept[...] = result
        return
    near_part = result[:, : 8 * HALF]
    lane = lax.broadcasted_iota(jnp.int32, near_part.shape, 1)
    kept[...] = jnp.where((lane < jnp.where(core == 0, 8 * HALF, HALF)), near_part, 0.0)
    to_z[...] = jnp.where(lane < HALF, 0.0, near_part).astype(bf16)
    to_y[...] = result[:, 8 * HALF :].astype(bf16)


def whole(shape):
    return pl.BlockSpec(shape, lambda i, role: (0,) * len(shape))


def cross(role, operands, before, tables, last):
    start = before is None
    count = operands[0].shape[1]
    args = [role, *operands]
    if not start:
        args.append(before)
    args += list(tables)
    in_vmem = pl.BlockSpec(memory_space=pltpu.VMEM)
    if last:
        out_shape = [
            jax.ShapeDtypeStruct((ROWS, 8 * HALF), f32),
            jax.ShapeDtypeStruct((ROWS, 8 * HALF), bf16),
            jax.ShapeDtypeStruct((ROWS, 4 * HALF), bf16),
        ]
        out_specs = [in_vmem] * 3
    else:
        out_shape = jax.ShapeDtypeStruct((ROWS, PLANES * HALF), f32)
        out_specs = in_vmem
    return pl.pallas_call(
        functools.partial(cross_kernel, start, last),
        in_specs=[pl.BlockSpec(memory_space=pltpu.SMEM)] + [in_vmem] * (len(args) - 1),
        out_specs=out_specs,
        out_shape=out_shape,
        scratch_shapes=[pltpu.VMEM((PLANES, HALF, 2 * NF), f32)],
        compiler_params=pltpu.CompilerParams(vmem_limit_bytes=VMEM),
        cost_estimate=pl.CostEstimate(
            flops=PLANES * 8 * count * HALF * NF,
            bytes_accessed=6 * count * HALF * 2 * NF * 2,
            transcendentals=0,
        ),
    )(*args)


def combine_kernel(role, kept, from_z, from_y, own, give):
    core = role[1]
    y = jnp.where(role[0] != core, from_y[...].astype(f32), 0.0)
    z = jnp.where((core != 0) & (role[2] == 0), from_z[...].astype(f32), 0.0)
    gap = jnp.zeros((ROWS, HALF), f32)
    placed = jnp.concatenate([gap, y[:, : 2 * HALF], gap, y[:, 2 * HALF :], gap, gap], axis=1)
    total = (kept[...] + z + placed).astype(bf16)
    first, second = total[:, : 4 * HALF].astype(f32), total[:, 4 * HALF :].astype(f32)
    own[...] = jnp.where(core == 0, first, second).astype(bf16)
    give[...] = jnp.where(core == 0, second, first).astype(bf16)


def combine(role, kept, from_z, from_y):
    part = jax.ShapeDtypeStruct((ROWS, 4 * HALF), bf16)
    return pl.pallas_call(
        combine_kernel,
        grid_spec=pltpu.PrefetchScalarGridSpec(
            num_scalar_prefetch=1,
            grid=(1,),
            in_specs=[whole(a.shape) for a in (kept, from_z, from_y)],
            out_specs=[whole(part.shape)] * 2,
        ),
        out_shape=[part, part],
        compiler_params=pltpu.CompilerParams(vmem_limit_bytes=VMEM),
        name="combine",
    )(role, kept, from_z, from_y)


def assemble_kernel(role, slots, own, got, out):
    core = role[1]
    mine, other = own[...].astype(f32), got[...].astype(f32)
    first = jnp.where(core == 0, mine, other)
    second = jnp.where(core == 0, other, mine)
    planes = [
        jnp.concatenate([first[:, i * HALF : (i + 1) * HALF], second[:, i * HALF : (i + 1) * HALF]], axis=1)
        for i in range(REACH)
    ]
    for slot in range(REACH):
        distance = slots[slot]
        value = jnp.zeros((ROWS, 2 * HALF), f32)
        for k in range(REACH):
            value = jnp.where(distance == k + 1, planes[k], value)
        out[:, slot * 2 * HALF : (slot + 1) * 2 * HALF] = value.astype(bf16)


def assemble(role, slots, own, got):
    shape = (ROWS, REACH * 2 * HALF)
    return pl.pallas_call(
        assemble_kernel,
        grid_spec=pltpu.PrefetchScalarGridSpec(
            num_scalar_prefetch=2,
            grid=(1,),
            in_specs=[pl.BlockSpec(own.shape, lambda i, *_: (0, 0)), pl.BlockSpec(got.shape, lambda i, *_: (0, 0))],
            out_specs=pl.BlockSpec(shape, lambda i, *_: (0, 0)),
        ),
        out_shape=jax.ShapeDtypeStruct(shape, bf16),
        compiler_params=pltpu.CompilerParams(vmem_limit_bytes=VMEM),
        name="assemble",
    )(role, slots, own, got)


def route(blocks, times, target):
    pairs = []
    for b in range(blocks):
        z, y_hi, core = b // 4, b // 2 % 2, b % 2
        for t in range(times):
            to_z, to_y, to_core, to_t = target(z, y_hi, core, t)
            if not 0 <= to_z < blocks // 4:
                to_z, to_core = z, 1 - core
            pairs.append((b * times + t, ((to_z * 2 + to_y) * 2 + to_core) * times + to_t))
    return pairs


def body(traces, valid_mask, pair_owner):
    blocks, times = lax.axis_size("chan"), lax.axis_size("tm")
    windows_all = traces.shape[1] * times

    def move(block, target):
        return lax.ppermute(block, ("chan", "tm"), route(blocks, times, target))

    def to_core(block):
        return move(block, lambda z, y, c, t: (z, y, 1 - c, t))

    reader = lax.axis_index("chan")
    core = reader % 2
    top = (reader // 4 == blocks // 4 - 1).astype(jnp.int32)
    places = jnp.arange(3, dtype=jnp.int32)
    role = jnp.where(places == 0, reader // 2 % 2, jnp.where(places == 1, core, top))
    slots = pair_owner[0] - reader
    forward, band = jnp.asarray(forward_table()), jnp.asarray(band_table())
    high, low = inverse_tables(windows_all)
    tables = (jnp.asarray(high), jnp.asarray(low))
    mask = valid_mask[0]

    rest = CHUNKS[0][1]
    later = traces.shape[1] - rest
    head, give = prepare(role, traces[0], mask, 0, rest)
    given_head = to_core(give)
    tail, give = prepare(role, traces[0], mask, rest, later)
    given_tail = to_core(give)
    sets = []
    order = role
    for k, (first, count) in enumerate(CHUNKS):
        if k == 0:
            own = whiten(order, head, given_head, forward, band, count, 0)
        else:
            own = whiten(order, tail, given_tail, forward, band, count, first - rest)
        own, order = lax.optimization_barrier((own, order))
        near = move(own, lambda z, y, c, t: (z - 1 + 2 * c, y, c, t))
        across = move(own, lambda z, y, c, t: (z, 1 - y, c, t) if y != c else (z, y, 1 - c, t))
        sets.append((own, near, across))
    stack = None
    for k, operands in enumerate(sets):
        stack = cross(order, operands, stack, tables, k == len(sets) - 1)
    kept, for_z, for_y = stack
    from_z = move(for_z, lambda z, y, c, t: (z + 1 - 2 * c, y, c, t))
    from_y = move(for_y, lambda z, y, c, t: (z, 1 - y, c, t) if y == c else (z, y, 1 - c, t))
    mine, give = combine(role, kept, from_z, from_y)
    partial = assemble(role, slots, mine, to_core(give))

    def exchange(block, bit):
        return move(block, lambda z, y, c, t: (z, y, c, t ^ bit)).astype(f32)

    partial = (partial.astype(f32) + exchange(partial, 4)).astype(bf16)
    far, third, near = (exchange(partial, bit) for bit in (2, 3, 1))
    partial = (partial.astype(f32) + near) + (far + third)
    result = partial[:LAGS].reshape(LAGS, REACH, 2 * HALF)
    return result.transpose(1, 0, 2)[None]


def solution(mesh):
    return jax.shard_map(
        body,
        mesh=mesh,
        in_specs=(P("chan", "tm", None, None), P("chan", "tm", None), P("chan", None)),
        out_specs=P("chan", None, None, None),
        check_vma=False,
    )
```
